32 devices in a mesh: groups: 2 (over y), row: 4 (over z), col: 4 (over x, core).
Axes of the slice: x: 2, y: 2, z: 4, core: 2. Of those that a mesh axis runs over, the one named last changes fastest.
Arguments:
- block_tiles: bfloat16 [8, 4, 128, 128, 128], P(('groups', 'row'), 'col'), parts along dimension 0, may hold values from -0.125 to 0.125
- tile_row: int32 [8, 4, 128], P(('groups', 'row'), 'col'), parts along dimension 0, may hold values from 0 to 11, as said below
- tile_col: int32 [8, 4, 128], P(('groups', 'row'), 'col'), parts along dimension 0, may hold values from 0 to 11, as said below
- tile_count: int32 [8, 4], P(('groups', 'row'), 'col'), parts along dimension 0, may hold values from 1 to 128, as said below
- objective: float32 [12288], P(('groups', 'col')), parts along dimension 0, may hold values from -6 to 6
- upper_bound: float32 [12288], P(('groups', 'col')), parts along dimension 0, may hold values from 0.5 to 4
- power_caps: float32 [64, 6144], P('groups', 'row'), parts along dimension 0, may hold values from -6 to 6
- primal_start: float32 [64, 6144], P('groups', 'col'), parts along dimension 0, may hold values from 0 to 0.5
- dual_start: float32 [64, 6144], P('groups', 'row'), parts along dimension 0, may hold values from 0 to 1
Outputs:
- primal_final: float32 [64, 6144], P('groups', 'col'), parts along dimension 0
- dual_final: float32 [64, 6144], P('groups', 'row'), parts along dimension 0
The draws below stay inside these ranges and needn't reach their ends.
There are 2 independent parts, one for each index of `groups`. The reference program is written for one: setup_inputs(seed, part) draws one part's arguments, and reference() takes and returns one part's arrays. A program takes and returns all parts, laid end to end along the dimension named above; each array names one. Nothing has to cross between parts.
Inputs may be any that keep to these rules, and one draw needn't show every extreme that they name: `tile_row`: constraint block of a slot, local to its row index. `tile_col`: variable block of a slot, local to its col index; the slots of one device name distinct pairs of (tile_row, tile_col). `tile_count`: some device of every draw has all 128 slots live; the busiest devices hold about three times the mean.
All inputs are finite; a program needn't handle non-finite values.
Results may differ from the reference program's by a relative error of at most 0.0011.
Values sent between devices are 32-bit elements; how exact they have to be, the bound alone decides.
A program may use at most 64 MiB of HBM per device.

```python
import math
import jax
import jax.numpy as jnp
from jax import lax

B = 128
S = 32
RB_DEV = 12
CB_DEV = 12
TILES = 128
ITERS = 6
NCON = 6144
NVAR = 6144
N_ROW = 4
N_COL = 4


def slot_positions(key):
    row_devs = NCON // (RB_DEV * B)
    col_devs = NVAR // (CB_DEV * B)
    subkeys = jax.random.split(jax.random.fold_in(key, 23), row_devs * col_devs)
    orders = jax.vmap(lambda single: jax.random.permutation(single, RB_DEV * CB_DEV))(subkeys)
    chosen = orders[:, :TILES].astype(jnp.int32).reshape(row_devs, col_devs, TILES)
    return chosen


def draw_tile_row(key, part):
    return (slot_positions(key) // CB_DEV).astype(jnp.int32)


def draw_tile_col(key, part):
    return (slot_positions(key) % CB_DEV).astype(jnp.int32)


def draw_tile_count(key, part):
    row_devs = NCON // (RB_DEV * B)
    col_devs = NVAR // (CB_DEV * B)
    first, second, third, fourth = jax.random.split(jax.random.fold_in(key, 41), 4)
    shape_two = (row_devs, col_devs)
    lower_count = jax.random.randint(first, shape_two, max(1, TILES // 6), max(1, TILES // 3) + 1)
    higher_count = jax.random.randint(second, shape_two, max(1, TILES // 2), TILES + 1)
    busy_flag = jax.random.randint(third, shape_two, 0, 8) == 0
    counts = jnp.where(busy_flag, higher_count, lower_count)
    full_device = jax.random.randint(fourth, (), 0, row_devs * col_devs)
    flat_index = jnp.arange(row_devs * col_devs, dtype=jnp.int32).reshape(shape_two)
    counts = jnp.where(flat_index == full_device, TILES, counts)
    return counts.astype(jnp.int32)


def steps_of(own_key, dims, cuts, low, high):
    loudness = 1.0
    for position, blocks in cuts:
        steps = jax.random.uniform(jax.random.fold_in(jax.random.fold_in(own_key, 6), position), (blocks,), jnp.float32, low / len(cuts), high / len(cuts))
        loudness = loudness * jnp.repeat(jnp.exp(steps), dims[position] // blocks).reshape((-1,) + (1,) * (len(dims) - 1 - position))
    return loudness


def centred(stream_key, extent, deviation, limit, cuts=(), kind=jnp.bfloat16):
    drawn = jax.random.normal(stream_key, extent, jnp.float32) * deviation
    if len(cuts) > 0:
        drawn = steps_of(stream_key, extent, cuts, -0.22, 0.18) * drawn
    return jnp.clip(drawn, min=-limit, max=limit).astype(kind)


def setup_inputs(seed: int = 0, part: int = 0) -> dict:
    key_of = jax.random.split(jax.random.key(seed), 10)
    part_keys = jax.random.split(jax.random.fold_in(key_of[9], part), 10)
    return {
        "block_tiles": centred(part_keys[0], (N_ROW, N_COL, TILES, B, B), (B * CB_DEV * N_COL // 3) ** -0.5, 0.125, ((0, 4), (1, 4))),
        "tile_row": draw_tile_row(jax.random.fold_in(jax.random.fold_in(key_of[9], part), 71), part),
        "tile_col": draw_tile_col(jax.random.fold_in(jax.random.fold_in(key_of[9], part), 71), part),
        "tile_count": draw_tile_count(jax.random.fold_in(jax.random.fold_in(key_of[9], part), 71), part),
        "objective": centred(part_keys[4], (NVAR,), 1.0, 6.0, ((0, 4),), jnp.float32),
        "upper_bound": jnp.clip(jnp.exp(math.log(4.0) - 2.0794415 * jax.random.uniform(part_keys[5], (NVAR,), jnp.float32) ** steps_of(part_keys[5], (NVAR,), ((0, 4),), -0.2, 0.2)), 0.5, 4.0),
        "power_caps": centred(part_keys[6], (S, NCON), 1.0, 6.0, ((1, 4),), jnp.float32),
        "primal_start": jnp.clip(0.5 * jax.random.uniform(part_keys[7], (S, NVAR), jnp.float32) ** steps_of(part_keys[7], (S, NVAR), ((1, 4),), -0.2, 0.2), 0.0, 0.5),
        "dual_start": jnp.clip(1.0 * jax.random.uniform(part_keys[8], (S, NCON), jnp.float32) ** steps_of(part_keys[8], (S, NCON), ((1, 4),), -0.2, 0.2), 0.0, 1.0),
    }


PRIMAL_STEP = 0.5
DUAL_STEP = 0.2


def live_table(tile_count):
    slots = jnp.arange(TILES, dtype=jnp.int32)
    return (slots[None, None, :] < tile_count[:, :, None]).astype(jnp.float32)


def adjoint_product(dual_low, block_tiles, tile_row, tile_col, live_slots):
    dual_four = dual_low.astype(jnp.float32).reshape(S, N_ROW, RB_DEV, B)
    columns = jnp.arange(CB_DEV, dtype=jnp.int32)

    def one_row(totals, row_index):
        dual_rows = dual_four[:, row_index]
        selected = dual_rows[:, tile_row[row_index]]
        product = jnp.einsum("sctb,ctbk->sctk", selected, block_tiles[row_index].astype(jnp.float32), precision=lax.Precision.HIGHEST)
        product = product * live_slots[row_index][None, :, :, None]
        onehot = (tile_col[row_index][:, :, None] == columns[None, None, :]).astype(jnp.float32)
        pieces = jnp.einsum("sctk,ctj->scjk", product, onehot, precision=lax.Precision.HIGHEST)
        return totals + pieces, None

    totals, _ = lax.scan(one_row, jnp.zeros((S, N_COL, CB_DEV, B), jnp.float32), jnp.arange(N_ROW, dtype=jnp.int32))
    return totals.reshape(S, NVAR)


def forward_product(extrap, block_tiles, tile_row, tile_col, live_slots):
    primal_four = extrap.astype(jnp.float32).reshape(S, N_COL, CB_DEV, B)
    col_index = jnp.arange(N_COL, dtype=jnp.int32)
    rows_local = jnp.arange(RB_DEV, dtype=jnp.int32)

    def one_row(carry_value, row_index):
        selected = primal_four[:, col_index[:, None], tile_col[row_index]]
        product = jnp.einsum("sctk,ctbk->sctb", selected, block_tiles[row_index].astype(jnp.float32), precision=lax.Precision.HIGHEST)
        product = product * live_slots[row_index][None, :, :, None]
        onehot = (tile_row[row_index][:, :, None] == rows_local[None, None, :]).astype(jnp.float32)
        pieces = jnp.einsum("sctb,ctj->sjb", product, onehot, precision=lax.Precision.HIGHEST)
        return carry_value, pieces

    _, stacked = lax.scan(one_row, jnp.zeros((), jnp.float32), jnp.arange(N_ROW, dtype=jnp.int32))
    return jnp.transpose(stacked, (1, 0, 2, 3)).reshape(S, NCON)


def reference(block_tiles, tile_row, tile_col, tile_count, objective, upper_bound, power_caps, primal_start, dual_start):
    live_slots = live_table(tile_count)
    primal = primal_start
    dual = dual_start
    for iteration in range(ITERS):
        dual_low = lax.optimization_barrier(dual.astype(jnp.bfloat16))
        adjoint = adjoint_product(dual_low, block_tiles, tile_row, tile_col, live_slots)
        primal_next = jnp.minimum(jnp.maximum(primal - PRIMAL_STEP * (objective[None, :] - adjoint), 0.0), upper_bound[None, :])
        extrap = lax.optimization_barrier((2.0 * primal_next - primal).astype(jnp.bfloat16))
        forward = forward_product(extrap, block_tiles, tile_row, tile_col, live_slots)
        dual = jnp.maximum(dual + DUAL_STEP * (power_caps - forward), 0.0)
        primal = primal_next
    return primal, dual
```

```python
import functools

import jax
import jax.numpy as jnp
from jax import lax
from jax.experimental import pallas as pl
from jax.experimental.pallas import tpu as pltpu
from jax.sharding import PartitionSpec as P

ITERS = 6


PRIMAL_STEP = 0.5
DUAL_STEP = 0.2

TILE_STEP = 16
MESH = pl.DeviceIdType.MESH


def build_kernel(step_slots, rows_ref, cols_ref, count_ref, tiles_ref, k_ref):
    block = tiles_ref.shape[1]
    k_per = k_ref.shape[2] // block
    step = pl.program_id(0)

    @pl.when(step == 0)
    def _():
        k_ref[...] = jnp.zeros_like(k_ref)

    for i in range(step_slots):
        slot = step * step_slots + i

        @pl.when(slot < count_ref[0])
        def _():
            row = rows_ref[slot]
            col = cols_ref[slot]
            row_at = pl.multiple_of(row * block, block)
            k_in = pl.multiple_of(lax.rem(col, k_per) * block, block)
            k_ref[lax.div(col, k_per), pl.ds(row_at, block), pl.ds(k_in, block)] = tiles_ref[i]


def build_dense(tiles, rows, cols, count, cons, nvar, k_chunks):
    slots, block = tiles.shape[0], tiles.shape[1]
    step_slots = TILE_STEP if slots % TILE_STEP == 0 else 1
    k_shape = (k_chunks, cons, nvar // k_chunks)
    return pl.pallas_call(
        functools.partial(build_kernel, step_slots),
        out_shape=jax.ShapeDtypeStruct(k_shape, tiles.dtype),
        grid_spec=pltpu.PrefetchScalarGridSpec(
            num_scalar_prefetch=3,
            grid=(slots // step_slots,),
            in_specs=[pl.BlockSpec((step_slots, block, block), lambda t, *_: (t, 0, 0))],
            out_specs=pl.BlockSpec(k_shape, lambda t, *_: (0, 0, 0)),
        ),
        compiler_params=pltpu.CompilerParams(vmem_limit_bytes=40 << 20),
        name="build_dense",
    )(rows, cols, count, tiles)


TILE_COPIES = 8


def pdhg_kernel(
    iters,
    block,
    rows_hbm,
    cols_hbm,
    count_hbm,
    tiles_hbm,
    d0_hbm,
    p0_hbm,
    obj_hbm,
    ub_hbm,
    caps_hbm,
    p_out,
    d_out,
    rows_ref,
    cols_ref,
    count_ref,
    where_ref,
    slot_of,
    tiles_ref,
    obj_ref,
    ub_ref,
    caps_ref,
    k_ref,
    kt_ref,
    obj_wide,
    ub_wide,
    primal,
    dual,
    part,
    part_got,
    fwd,
    fwd_got,
    part_send,
    part_recv,
    pri_send,
    pri_recv,
    fwd_send,
    fwd_recv,
    dua_send,
    dua_recv,
    slot_sem,
    tile_sem,
    start_sem,
    vec_sem,
    where_sem,
):
    batches, _, rows, half_v = part.shape
    half = fwd.shape[3]
    cons = k_ref.shape[1]
    r = lax.axis_index("row")
    c = lax.axis_index("col")
    core, chip = lax.rem(c, 2), lax.div(c, 2)
    other = 1 - core
    sibling = chip * 2 + other
    across = (1 - chip) * 2 + core
    diagonal = (1 - chip) * 2 + other
    near = lax.div(r, 2)
    far = 1 - near
    inner = jnp.logical_or(r == 1, r == 2)
    outer = jnp.logical_not(inner)
    near_owner, far_owner = 1 + near, 1 + far
    near_end, far_end = 3 * near, 3 * far

    barrier = pltpu.get_barrier_semaphore()
    for k in range(1, 4):
        pl.semaphore_signal(
            barrier, inc=1, device_id={"row": lax.rem(r + k, 4)}, device_id_type=MESH
        )
        pl.semaphore_signal(
            barrier, inc=1, device_id={"col": lax.rem(c + k, 4)}, device_id_type=MESH
        )

    def rows_of(b):
        return slice(b * rows, (b + 1) * rows)

    def remote(axis, peer, src, dst, send, recv):
        return pltpu.make_async_remote_copy(
            src_ref=src,
            dst_ref=dst,
            send_sem=send,
            recv_sem=recv,
            device_id={axis: peer},
            device_id_type=MESH,
        )

    def part_copy(b, which, place):
        q, owner = ((near, near_owner), (far, far_owner))[which]
        return remote(
            "row", owner, part.at[b, q], part_got.at[b, place],
            part_send.at[b, which], part_recv.at[b, place],
        )

    def pri_copy(b, k, s):
        peer = (far_end, far_owner, near_end)[k]
        return remote(
            "row", peer, primal.at[s, b, near], primal.at[s, b, near],
            pri_send.at[b, k], pri_recv.at[b, near],
        )

    def pri_arrived(b, q, s):
        pltpu.make_async_remote_copy(
            src_ref=primal.at[s, b, q],
            dst_ref=primal.at[s, b, q],
            send_sem=pri_send.at[b, 0],
            recv_sem=pri_recv.at[b, q],
            device_id={"row": far_owner},
            device_id_type=MESH,
        ).wait_recv()

    def fwd_copy(b, k, s):
        peer, q = ((sibling, other), (across, core), (diagonal, other))[k]
        return remote(
            "col", peer, fwd.at[b, q], fwd_got.at[s, b, k],
            fwd_send.at[b, k], fwd_recv.at[s, b, k],
        )

    def dua_copy(b):
        return remote(
            "col", sibling, dual.at[b, core], dual.at[b, core], dua_send.at[b], dua_recv.at[b]
        )

    def send_far(b):
        @pl.when(inner)
        def _():
            part_copy(b, 1, 1).start()

        @pl.when(outer)
        def _():
            part_copy(b, 1, 2).start()

    def send_near(b):
        @pl.when(outer)
        def _():
            part_copy(b, 0, 0).start()

    def adjoint(b, s, first=False, send=True):
        if not first:
            dua_copy(b).wait()
        low = jnp.concatenate([dual[b, 0], dual[b, 1]], axis=1).astype(jnp.bfloat16)
        part[b, far] = jnp.dot(low, k_ref[far], preferred_element_type=jnp.float32)
        if send:
            send_far(b)
        part[b, near] = jnp.dot(low, k_ref[near], preferred_element_type=jnp.float32)
        if send:
            send_near(b)

    def primal_step(b, s):
        @pl.when(inner)
        def _():
            part_copy(b, 0, 0).wait_recv()
            part_copy(b, 0, 1).wait_recv()
            part_copy(b, 0, 2).wait_recv()
            total = (part[b, near] + part_got[b, 0]) + (part_got[b, 1] + part_got[b, 2])
            primal[s, b, near] = jnp.minimum(
                jnp.maximum(
                    primal[1 - s, b, near] - PRIMAL_STEP * (obj_wide[near] - total), 0.0
                ),
                ub_wide[near],
            )
            for k in range(3):
                pri_copy(b, k, s).start()
            part_copy(b, 1, 1).wait_send()

        @pl.when(outer)
        def _():
            part_copy(b, 1, 2).wait_send()
            part_copy(b, 0, 0).wait_send()

    def forward(b, s):
        @pl.when(outer)
        def _():
            pri_arrived(b, near, s)

        @pl.when(inner)
        def _():
            for k in range(3):
                pri_copy(b, k, s).wait_send()

        def low(q):
            return (2.0 * primal[s, b, q] - primal[1 - s, b, q]).astype(jnp.bfloat16)

        pri_arrived(b, far, s)
        both = [low(near), low(far)]
        sums = [
            sum(
                jnp.dot(part_low, kt_ref[q, v], preferred_element_type=jnp.float32)
                for part_low, v in zip(both, (near, far))
            )
            for q in (other, core)
        ]
        fwd[b, other] = sums[0]
        fwd[b, core] = sums[1]
        for k in (2, 0, 1):
            fwd_copy(b, k, s).start()

    own = pl.ds(pl.multiple_of(core * half, 128), half)

    def dual_step(b, s):
        for k in range(3):
            fwd_copy(b, k, s).wait()
        total = (fwd[b, core] + fwd_got[s, b, 0]) + (fwd_got[s, b, 1] + fwd_got[s, b, 2])
        dual[b, core] = jnp.maximum(
            dual[b, core] + DUAL_STEP * (caps_ref[rows_of(b), own] - total), 0.0
        )
        dua_copy(b).start()

    row_blocks, per_half, per_half_v = cons // block, half // block, half_v // block
    col_blocks = 2 * per_half_v
    slots = tiles_hbm.shape[0]

    def transpose_rows(first, last):
        def one(i, carry):
            at = pl.multiple_of(i * block, block)
            into = pl.multiple_of(lax.rem(i, per_half) * block, block)
            for j in range(col_blocks):
                inside = slice(j % per_half_v * block, (j % per_half_v + 1) * block)
                kt_ref[lax.div(i, per_half), j // per_half_v, inside, pl.ds(into, block)] = (
                    k_ref[j // per_half_v, pl.ds(at, block), inside].T
                )
            return carry

        lax.fori_loop(first, last, one, 0)

    def fetch(src, dst, sem):
        copy = pltpu.make_async_copy(src, dst, sem)
        copy.start()
        return copy

    slot_copies = [
        fetch(src, dst, slot_sem.at[i])
        for i, (src, dst) in enumerate(
            ((rows_hbm, rows_ref), (cols_hbm, cols_ref), (count_hbm, count_ref))
        )
    ]
    share = slots // TILE_COPIES
    tile_copies = [
        fetch(tiles_hbm.at[pl.ds(i * share, share)], tiles_ref.at[pl.ds(i * share, share)], tile_sem.at[i])
        for i in range(TILE_COPIES)
    ]
    start_copies = []
    for b in range(batches):
        for q in range(2):
            for i, (src, dst, width) in enumerate(((d0_hbm, dual, half), (p0_hbm, primal.at[1], half_v))):
                start_copies.append(
                    fetch(
                        src.at[pl.ds(b * rows, rows), pl.ds(q * width, width)],
                        dst.at[b, q],
                        start_sem.at[i, b, q],
                    )
                )
    vec_copies = [
        fetch(src, dst, vec_sem.at[i])
        for i, (src, dst) in enumerate(((obj_hbm, obj_ref), (ub_hbm, ub_ref), (caps_hbm, caps_ref)))
    ]

    tiles_ref[slots] = jnp.zeros_like(tiles_ref[slots])
    for copy in slot_copies:
        copy.wait()
    lane = lax.broadcasted_iota(jnp.int32, (slots, 128), 1)
    slot = lax.broadcasted_iota(jnp.int32, (slots, 128), 0)
    place = rows_ref[...] * col_blocks + cols_ref[...]
    place = jnp.where(lane[:1] < count_ref[...], place, -1)
    place = jnp.broadcast_to(place, (128, slots)).T
    for g in range(where_ref.shape[0]):
        found = jnp.where(place == lane + 128 * g, slot, slots)
        where_ref[g : g + 1, :] = jnp.min(found, axis=0, keepdims=True)
    where_copy = fetch(where_ref, slot_of, where_sem)
    for copy in tile_copies:
        copy.wait()
    where_copy.wait()

    def build_rows(i, carry):
        at = pl.ds(pl.multiple_of(i * block, block), block)
        for j in range(col_blocks):
            index = i * col_blocks + j
            inside = slice(j % per_half_v * block, (j % per_half_v + 1) * block)
            k_ref[j // per_half_v, at, inside] = tiles_ref[
                slot_of[lax.div(index, 128), lax.rem(index, 128)]
            ]
        return carry

    lax.fori_loop(0, row_blocks, build_rows, 0)
    for copy in start_copies:
        copy.wait()

    def transpose_third(i, s):
        transpose_rows(i * row_blocks // 3, (i + 1) * row_blocks // 3)

    stages = {
        "A": adjoint, "B": primal_step, "C": forward, "D": dual_step, "T": transpose_third
    }

    def run(order, s):
        for step in order:
            now = s if step[0].isupper() else 1 - s
            stages[step[0].upper()](int(step[1]), now)

    for b in range(batches):
        adjoint(b, 0, True, b > 1)
        if b == 1:
            pl.semaphore_wait(barrier, 6)
            for a in range(2):
                send_far(a)
                send_near(a)
    for copy in vec_copies:
        copy.wait()
    for j in range(col_blocks):
        at = slice(j % per_half_v * block, (j % per_half_v + 1) * block)
        obj_wide[j // per_half_v, :, at] = jnp.broadcast_to(obj_ref[j : j + 1, :], (rows, block))
        ub_wide[j // per_half_v, :, at] = jnp.broadcast_to(ub_ref[j : j + 1, :], (rows, block))
    run(FIRST, 0)

    def body(t, carry):
        run(EVERY, lax.rem(t, 2))
        return carry

    lax.fori_loop(1, iters, body, 0)
    run(LAST, iters % 2)

    final = (iters - 1) % 2
    for b in range(batches):
        for q in range(2):
            p_out[rows_of(b), q * half_v : (q + 1) * half_v] = primal[final, b, q]
        dua_copy(b).wait()
        for q in range(2):
            d_out[rows_of(b), q * half : (q + 1) * half] = dual[b, q]


FIRST = ("T0", "B0", "T1", "B1", "T2", "B2", "C0", "B3", "C1", "D0", "C2")
EVERY = ("A0", "d1", "c3", "A1", "d2", "B0", "A2", "d3", "B1", "A3", "B2", "C0", "B3", "C1", "D0", "C2")
LAST = ("d1", "c3", "d2", "d3")


def pdhg(
    tiles, rows, cols, count, objective, upper_bound, power_caps, primal_start, dual_start
):
    slots, block = tiles.shape[0], tiles.shape[1]
    scenarios, nvar = primal_start.shape
    cons = dual_start.shape[1]
    half, half_v = cons // 2, nvar // 2
    batches, rows_batch = 4, scenarios // 4
    places = pl.cdiv((cons // block) * (nvar // block), 128)
    hbm = pl.BlockSpec(memory_space=pltpu.HBM)
    vmem = pl.BlockSpec(memory_space=pltpu.VMEM)
    f32 = jnp.float32
    var_shape = (batches, 2, rows_batch, half_v)
    con_shape = (batches, 2, rows_batch, half)
    dma = pltpu.SemaphoreType.DMA
    outs = pl.pallas_call(
        functools.partial(pdhg_kernel, ITERS, block),
        out_shape=(pltpu.VMEM((scenarios, nvar), f32), pltpu.VMEM((scenarios, cons), f32)),
        in_specs=[hbm] * 9,
        out_specs=(vmem, vmem),
        scratch_shapes=[
            pltpu.VMEM(rows.shape, rows.dtype),
            pltpu.VMEM(cols.shape, cols.dtype),
            pltpu.VMEM(count.shape, count.dtype),
            pltpu.VMEM((places, 128), jnp.int32),
            pltpu.SMEM((places, 128), jnp.int32),
            pltpu.VMEM((slots + 1, block, block), tiles.dtype),
            pltpu.VMEM((nvar // block, block), f32),
            pltpu.VMEM((nvar // block, block), f32),
            pltpu.VMEM(power_caps.shape, f32),
            pltpu.VMEM((2, cons, half_v), tiles.dtype),
            pltpu.VMEM((2, 2, half_v, half), tiles.dtype),
            pltpu.VMEM((2, rows_batch, half_v), f32),
            pltpu.VMEM((2, rows_batch, half_v), f32),
            pltpu.VMEM((2, *var_shape), f32),
            pltpu.VMEM(con_shape, f32),
            pltpu.VMEM(var_shape, f32),
            pltpu.VMEM((batches, 3, rows_batch, half_v), f32),
            pltpu.VMEM(con_shape, f32),
            pltpu.VMEM((2, batches, 3, rows_batch, half), f32),
            dma((batches, 2)),
            dma((batches, 3)),
            dma((batches, 3)),
            dma((batches, 2)),
            dma((batches, 3)),
            dma((2, batches, 3)),
            dma((batches,)),
            dma((batches,)),
            dma((3,)),
            dma((TILE_COPIES,)),
            dma((2, batches, 2)),
            dma((3,)),
            dma,
        ],
        compiler_params=pltpu.CompilerParams(
            collective_id=0, has_side_effects=True, vmem_limit_bytes=60 << 20
        ),
        name="pdhg",
    )(
        rows,
        cols,
        count,
        tiles,
        dual_start,
        primal_start,
        objective.reshape(-1, block),
        upper_bound.reshape(-1, block),
        power_caps,
    )
    return pl.pallas_call(
        store_kernel,
        out_shape=(
            jax.ShapeDtypeStruct((scenarios, nvar), f32),
            jax.ShapeDtypeStruct((scenarios, cons), f32),
        ),
        in_specs=[vmem] * 2,
        out_specs=(hbm, hbm),
        scratch_shapes=[dma((2,))],
        compiler_params=pltpu.CompilerParams(vmem_limit_bytes=4 << 20),
        name="store",
    )(*outs)


def store_kernel(p_ref, d_ref, p_out, d_out, sem):
    copies = [
        pltpu.make_async_copy(src, dst, sem.at[i])
        for i, (src, dst) in enumerate(((p_ref, p_out), (d_ref, d_out)))
    ]
    for copy in copies:
        copy.start()
    for copy in copies:
        copy.wait()


def pdhg_summed(dense, objective, upper_bound, power_caps, primal, dual):
    for _ in range(ITERS):
        part = jnp.dot(dual.astype(jnp.bfloat16), dense[0], preferred_element_type=jnp.float32)
        adjoint = lax.psum(part, "row")
        new = jnp.minimum(
            jnp.maximum(primal - PRIMAL_STEP * (objective[None, :] - adjoint), 0.0),
            upper_bound[None, :],
        )
        extrap = (2.0 * new - primal).astype(jnp.bfloat16)
        part = jnp.dot(extrap, dense[0].T, preferred_element_type=jnp.float32)
        forward = lax.psum(part, "col")
        dual = jnp.maximum(dual + DUAL_STEP * (power_caps - forward), 0.0)
        primal = new
    return primal, dual


def per_device(
    n_row,
    n_col,
    block_tiles,
    tile_row,
    tile_col,
    tile_count,
    objective,
    upper_bound,
    power_caps,
    primal_start,
    dual_start,
):
    block = block_tiles.shape[-1]
    cons = dual_start.shape[1]
    nvar = primal_start.shape[1]
    slots = block_tiles.shape[2]
    vectors = (objective, upper_bound, power_caps, primal_start, dual_start)
    if (
        (n_row, n_col) == (4, 4)
        and (slots, block) == (128, 128)
        and primal_start.shape[0] % 32 == 0
        and cons % (2 * block) == 0
        and nvar % (2 * block) == 0
    ):
        return pdhg(block_tiles[0, 0], tile_row[0], tile_col[0], tile_count, *vectors)
    dense = build_dense(
        block_tiles[0, 0], tile_row[0, 0], tile_col[0, 0], tile_count[0], cons, nvar, 1
    )
    return pdhg_summed(dense, *vectors)


def solution(mesh):
    return jax.shard_map(
        functools.partial(per_device, mesh.shape["row"], mesh.shape["col"]),
        mesh=mesh,
        in_specs=(
            P(("groups", "row"), "col", None, None, None),
            P(("groups", "row"), "col", None),
            P(("groups", "row"), "col", None),
            P(("groups", "row"), "col"),
            P(("groups", "col")),
            P(("groups", "col")),
            P("groups", "row"),
            P("groups", "col"),
            P("groups", "row"),
        ),
        out_specs=(P("groups", "col"), P("groups", "row")),
        check_vma=False,
    )
```

```python
import functools
import types

import jax
import jax.numpy as jnp
from jax import lax
from jax.experimental import pallas as pl
from jax.experimental.pallas import tpu as pltpu
from jax.sharding import PartitionSpec as P

ITERS = 6


PRIMAL_STEP = 0.5
DUAL_STEP = 0.2

TILE_STEP = 16
MESH = pl.DeviceIdType.MESH


def build_kernel(step_slots, rows_ref, cols_ref, count_ref, tiles_ref, k_ref):
    block = tiles_ref.shape[1]
    k_per = k_ref.shape[2] // block
    step = pl.program_id(0)

    @pl.when(step == 0)
    def _():
        k_ref[...] = jnp.zeros_like(k_ref)

    for i in range(step_slots):
        slot = step * step_slots + i

        @pl.when(slot < count_ref[0])
        def _():
            row = rows_ref[slot]
            col = cols_ref[slot]
            row_at = pl.multiple_of(row * block, block)
            k_in = pl.multiple_of(lax.rem(col, k_per) * block, block)
            k_ref[lax.div(col, k_per), pl.ds(row_at, block), pl.ds(k_in, block)] = tiles_ref[i]


def build_dense(tiles, rows, cols, count, cons, nvar, k_chunks):
    slots, block = tiles.shape[0], tiles.shape[1]
    step_slots = TILE_STEP if slots % TILE_STEP == 0 else 1
    k_shape = (k_chunks, cons, nvar // k_chunks)
    return pl.pallas_call(
        functools.partial(build_kernel, step_slots),
        out_shape=jax.ShapeDtypeStruct(k_shape, tiles.dtype),
        grid_spec=pltpu.PrefetchScalarGridSpec(
            num_scalar_prefetch=3,
            grid=(slots // step_slots,),
            in_specs=[pl.BlockSpec((step_slots, block, block), lambda t, *_: (t, 0, 0))],
            out_specs=pl.BlockSpec(k_shape, lambda t, *_: (0, 0, 0)),
        ),
        compiler_params=pltpu.CompilerParams(vmem_limit_bytes=40 << 20),
        name="build_dense",
    )(rows, cols, count, tiles)


TILE_COPIES = 8


def pdhg_kernel(
    iters,
    block,
    rows_hbm,
    cols_hbm,
    count_hbm,
    tiles_hbm,
    d0_hbm,
    p0_hbm,
    obj_hbm,
    ub_hbm,
    caps_hbm,
    p_out,
    d_out,
    rows_ref,
    cols_ref,
    count_ref,
    where_ref,
    slot_of,
    tiles_ref,
    obj_ref,
    ub_ref,
    caps_ref,
    k_ref,
    kt_ref,
    obj_wide,
    ub_wide,
    primal,
    dual,
    part,
    part_got,
    fwd,
    fwd_got,
    part_send,
    part_recv,
    pri_send,
    pri_recv,
    fwd_send,
    fwd_recv,
    dua_send,
    dua_recv,
    slot_sem,
    tile_sem,
    start_sem,
    vec_sem,
    where_sem,
):
    batches, _, rows, half_v = part.shape
    half = fwd.shape[3]
    cons = k_ref.shape[1]
    r = lax.axis_index("row")
    c = lax.axis_index("col")
    core, chip = lax.rem(c, 2), lax.div(c, 2)
    other = 1 - core
    sibling = chip * 2 + other
    across = (1 - chip) * 2 + core
    diagonal = (1 - chip) * 2 + other
    near = lax.div(r, 2)
    far = 1 - near
    inner = jnp.logical_or(r == 1, r == 2)
    outer = jnp.logical_not(inner)
    near_owner, far_owner = 1 + near, 1 + far
    near_end, far_end = 3 * near, 3 * far

    barrier = pltpu.get_barrier_semaphore()
    for k in range(1, 4):
        pl.semaphore_signal(
            barrier, inc=1, device_id={"row": lax.rem(r + k, 4)}, device_id_type=MESH
        )
        pl.semaphore_signal(
            barrier, inc=1, device_id={"col": lax.rem(c + k, 4)}, device_id_type=MESH
        )

    def rows_of(b):
        return slice(b * rows, (b + 1) * rows)

    def remote(axis, peer, src, dst, send, recv):
        width = src.shape[1]
        piece = width // 2

        def copy(at):
            return pltpu.make_async_remote_copy(
                src_ref=src.at[:, at],
                dst_ref=dst.at[:, at],
                send_sem=send,
                recv_sem=recv,
                device_id={axis: peer},
                device_id_type=MESH,
            )

        def start():
            for i in range(2):
                copy(pl.ds(i * piece, piece)).start()

        def whole():
            return copy(pl.ds(0, width))

        return types.SimpleNamespace(
            start=start,
            wait=lambda: whole().wait(),
            wait_send=lambda: whole().wait_send(),
            wait_recv=lambda: whole().wait_recv(),
        )

    def part_copy(b, which, place):
        q, owner = ((near, near_owner), (far, far_owner))[which]
        return remote(
            "row", owner, part.at[b, q], part_got.at[b, place],
            part_send.at[b, which], part_recv.at[b, place],
        )

    def pri_copy(b, k, s):
        peer = (far_end, far_owner, near_end)[k]
        return remote(
            "row", peer, primal.at[s, b, near], primal.at[s, b, near],
            pri_send.at[b, k], pri_recv.at[b, near],
        )

    def pri_arrived(b, q, s):
        pltpu.make_async_remote_copy(
            src_ref=primal.at[s, b, q],
            dst_ref=primal.at[s, b, q],
            send_sem=pri_send.at[b, 0],
            recv_sem=pri_recv.at[b, q],
            device_id={"row": far_owner},
            device_id_type=MESH,
        ).wait_recv()

    def fwd_copy(b, k, s):
        peer, q = ((sibling, other), (across, core), (diagonal, other))[k]
        return remote(
            "col", peer, fwd.at[b, q], fwd_got.at[s, b, k],
            fwd_send.at[b, k], fwd_recv.at[s, b, k],
        )

    def dua_copy(b):
        return remote(
            "col", sibling, dual.at[b, core], dual.at[b, core], dua_send.at[b], dua_recv.at[b]
        )

    def send_far(b):
        @pl.when(inner)
        def _():
            part_copy(b, 1, 1).start()

        @pl.when(outer)
        def _():
            part_copy(b, 1, 2).start()

    def send_near(b):
        @pl.when(outer)
        def _():
            part_copy(b, 0, 0).start()

    def adjoint(b, s, first=False):
        if not first:
            dua_copy(b).wait()
        low = jnp.concatenate([dual[b, 0], dual[b, 1]], axis=1).astype(jnp.bfloat16)
        part[b, far] = jnp.dot(low, k_ref[far], preferred_element_type=jnp.float32)
        send_far(b)
        part[b, near] = jnp.dot(low, k_ref[near], preferred_element_type=jnp.float32)
        send_near(b)

    def primal_step(b, s):
        @pl.when(inner)
        def _():
            part_copy(b, 0, 0).wait_recv()
            part_copy(b, 0, 1).wait_recv()
            part_copy(b, 0, 2).wait_recv()
            total = (part[b, near] + part_got[b, 0]) + (part_got[b, 1] + part_got[b, 2])
            primal[s, b, near] = jnp.minimum(
                jnp.maximum(
                    primal[1 - s, b, near] - PRIMAL_STEP * (obj_wide[near] - total), 0.0
                ),
                ub_wide[near],
            )
            for k in range(3):
                pri_copy(b, k, s).start()
            part_copy(b, 1, 1).wait_send()

        @pl.when(outer)
        def _():
            part_copy(b, 1, 2).wait_send()
            part_copy(b, 0, 0).wait_send()

    def forward(b, s):
        @pl.when(outer)
        def _():
            pri_arrived(b, near, s)

        @pl.when(inner)
        def _():
            for k in range(3):
                pri_copy(b, k, s).wait_send()

        def low(q):
            return (2.0 * primal[s, b, q] - primal[1 - s, b, q]).astype(jnp.bfloat16)

        pri_arrived(b, far, s)
        both = [low(near), low(far)]
        sums = [
            sum(
                jnp.dot(part_low, kt_ref[q, v], preferred_element_type=jnp.float32)
                for part_low, v in zip(both, (near, far))
            )
            for q in (other, core)
        ]
        fwd[b, other] = sums[0]
        fwd[b, core] = sums[1]
        for k in (2, 0, 1):
            fwd_copy(b, k, s).start()

    own = pl.ds(pl.multiple_of(core * half, 128), half)

    def dual_step(b, s):
        for k in range(3):
            fwd_copy(b, k, s).wait()
        total = (fwd[b, core] + fwd_got[s, b, 0]) + (fwd_got[s, b, 1] + fwd_got[s, b, 2])
        dual[b, core] = jnp.maximum(
            dual[b, core] + DUAL_STEP * (caps_ref[rows_of(b), own] - total), 0.0
        )
        dua_copy(b).start()

    row_blocks, per_half, per_half_v = cons // block, half // block, half_v // block
    col_blocks = 2 * per_half_v
    slots = tiles_hbm.shape[0]

    def transpose_rows(first, last):
        def one(i, carry):
            at = pl.multiple_of(i * block, block)
            into = pl.multiple_of(lax.rem(i, per_half) * block, block)
            for j in range(col_blocks):
                inside = slice(j % per_half_v * block, (j % per_half_v + 1) * block)
                kt_ref[lax.div(i, per_half), j // per_half_v, inside, pl.ds(into, block)] = (
                    k_ref[j // per_half_v, pl.ds(at, block), inside].T
                )
            return carry

        lax.fori_loop(first, last, one, 0)

    def fetch(src, dst, sem):
        copy = pltpu.make_async_copy(src, dst, sem)
        copy.start()
        return copy

    slot_copies = [
        fetch(src, dst, slot_sem.at[i])
        for i, (src, dst) in enumerate(
            ((rows_hbm, rows_ref), (cols_hbm, cols_ref), (count_hbm, count_ref))
        )
    ]
    share = slots // TILE_COPIES
    tile_copies = [
        fetch(tiles_hbm.at[pl.ds(i * share, share)], tiles_ref.at[pl.ds(i * share, share)], tile_sem.at[i])
        for i in range(TILE_COPIES)
    ]
    start_copies = []
    for b in range(batches):
        for q in range(2):
            for i, (src, dst, width) in enumerate(((d0_hbm, dual, half), (p0_hbm, primal.at[1], half_v))):
                start_copies.append(
                    fetch(
                        src.at[pl.ds(b * rows, rows), pl.ds(q * width, width)],
                        dst.at[b, q],
                        start_sem.at[i, b, q],
                    )
                )
    vec_copies = [
        fetch(src, dst, vec_sem.at[i])
        for i, (src, dst) in enumerate(((obj_hbm, obj_ref), (ub_hbm, ub_ref), (caps_hbm, caps_ref)))
    ]

    tiles_ref[slots] = jnp.zeros_like(tiles_ref[slots])
    for copy in slot_copies:
        copy.wait()
    lane = lax.broadcasted_iota(jnp.int32, (slots, 128), 1)
    slot = lax.broadcasted_iota(jnp.int32, (slots, 128), 0)
    place = rows_ref[...] * col_blocks + cols_ref[...]
    place = jnp.where(lane[:1] < count_ref[...], place, -1)
    place = jnp.broadcast_to(place, (128, slots)).T
    for g in range(where_ref.shape[0]):
        found = jnp.where(place == lane + 128 * g, slot, slots)
        where_ref[g : g + 1, :] = jnp.min(found, axis=0, keepdims=True)
    where_copy = fetch(where_ref, slot_of, where_sem)
    for copy in tile_copies:
        copy.wait()
    where_copy.wait()

    def build_rows(i, carry):
        at = pl.ds(pl.multiple_of(i * block, block), block)
        for j in range(col_blocks):
            index = i * col_blocks + j
            inside = slice(j % per_half_v * block, (j % per_half_v + 1) * block)
            k_ref[j // per_half_v, at, inside] = tiles_ref[
                slot_of[lax.div(index, 128), lax.rem(index, 128)]
            ]
        return carry

    lax.fori_loop(0, row_blocks, build_rows, 0)
    for copy in start_copies:
        copy.wait()

    def transpose_part(i, s):
        transpose_rows(i * row_blocks // 6, (i + 1) * row_blocks // 6)

    def primal_out(i, s):
        for b in range(batches):
            for q in range(2):
                p_out[rows_of(b), q * half_v : (q + 1) * half_v] = primal[s, b, q]

    stages = {
        "P": primal_out, "A": adjoint, "B": primal_step, "C": forward, "D": dual_step, "T": transpose_part
    }

    def run(order, s):
        for step in order:
            now = s if step[0].isupper() else 1 - s
            stages[step[0].upper()](int(step[1]), now)

    pl.semaphore_wait(barrier, 6)
    for b in range(batches):
        adjoint(b, 0, True)
    for copy in vec_copies:
        copy.wait()
    for j in range(col_blocks):
        at = slice(j % per_half_v * block, (j % per_half_v + 1) * block)
        obj_wide[j // per_half_v, :, at] = jnp.broadcast_to(obj_ref[j : j + 1, :], (rows, block))
        ub_wide[j // per_half_v, :, at] = jnp.broadcast_to(ub_ref[j : j + 1, :], (rows, block))
    run(FIRST, 0)

    def body(t, carry):
        run(EVERY, lax.rem(t, 2))
        return carry

    lax.fori_loop(1, iters, body, 0)
    run(LAST, iters % 2)

    for b in range(batches):
        dua_copy(b).wait()
        for q in range(2):
            d_out[rows_of(b), q * half : (q + 1) * half] = dual[b, q]


FIRST = ("T0", "T1", "B0", "T2", "T3", "B1", "T4", "T5", "B2", "C0", "B3", "C1", "D0", "C2")
EVERY = ("A0", "d1", "c3", "A1", "d2", "B0", "A2", "d3", "B1", "A3", "C0", "B2", "C1", "B3", "D0", "C2")
LAST = ("d1", "c3", "p0", "d2", "d3")


def pdhg(
    tiles, rows, cols, count, objective, upper_bound, power_caps, primal_start, dual_start
):
    slots, block = tiles.shape[0], tiles.shape[1]
    scenarios, nvar = primal_start.shape
    cons = dual_start.shape[1]
    half, half_v = cons // 2, nvar // 2
    batches, rows_batch = 4, scenarios // 4
    places = pl.cdiv((cons // block) * (nvar // block), 128)
    hbm = pl.BlockSpec(memory_space=pltpu.HBM)
    vmem = pl.BlockSpec(memory_space=pltpu.VMEM)
    f32 = jnp.float32
    var_shape = (batches, 2, rows_batch, half_v)
    con_shape = (batches, 2, rows_batch, half)
    dma = pltpu.SemaphoreType.DMA
    outs = pl.pallas_call(
        functools.partial(pdhg_kernel, ITERS, block),
        out_shape=(pltpu.VMEM((scenarios, nvar), f32), pltpu.VMEM((scenarios, cons), f32)),
        in_specs=[hbm] * 9,
        out_specs=(vmem, vmem),
        scratch_shapes=[
            pltpu.VMEM(rows.shape, rows.dtype),
            pltpu.VMEM(cols.shape, cols.dtype),
            pltpu.VMEM(count.shape, count.dtype),
            pltpu.VMEM((places, 128), jnp.int32),
            pltpu.SMEM((places, 128), jnp.int32),
            pltpu.VMEM((slots + 1, block, block), tiles.dtype),
            pltpu.VMEM((nvar // block, block), f32),
            pltpu.VMEM((nvar // block, block), f32),
            pltpu.VMEM(power_caps.shape, f32),
            pltpu.VMEM((2, cons, half_v), tiles.dtype),
            pltpu.VMEM((2, 2, half_v, half), tiles.dtype),
            pltpu.VMEM((2, rows_batch, half_v), f32),
            pltpu.VMEM((2, rows_batch, half_v), f32),
            pltpu.VMEM((2, *var_shape), f32),
            pltpu.VMEM(con_shape, f32),
            pltpu.VMEM(var_shape, f32),
            pltpu.VMEM((batches, 3, rows_batch, half_v), f32),
            pltpu.VMEM(con_shape, f32),
            pltpu.VMEM((2, batches, 3, rows_batch, half), f32),
            dma((batches, 2)),
            dma((batches, 3)),
            dma((batches, 3)),
            dma((batches, 2)),
            dma((batches, 3)),
            dma((2, batches, 3)),
            dma((batches,)),
            dma((batches,)),
            dma((3,)),
            dma((TILE_COPIES,)),
            dma((2, batches, 2)),
            dma((3,)),
            dma,
        ],
        compiler_params=pltpu.CompilerParams(
            collective_id=0, has_side_effects=True, vmem_limit_bytes=60 << 20
        ),
        name="pdhg",
    )(
        rows,
        cols,
        count,
        tiles,
        dual_start,
        primal_start,
        objective.reshape(-1, block),
        upper_bound.reshape(-1, block),
        power_caps,
    )
    return pl.pallas_call(
        store_kernel,
        out_shape=(
            jax.ShapeDtypeStruct((scenarios, nvar), f32),
            jax.ShapeDtypeStruct((scenarios, cons), f32),
        ),
        in_specs=[vmem] * 2,
        out_specs=(hbm, hbm),
        scratch_shapes=[dma((2,))],
        compiler_params=pltpu.CompilerParams(vmem_limit_bytes=4 << 20),
        name="store",
    )(*outs)


def store_kernel(p_ref, d_ref, p_out, d_out, sem):
    copies = [
        pltpu.make_async_copy(src, dst, sem.at[i])
        for i, (src, dst) in enumerate(((p_ref, p_out), (d_ref, d_out)))
    ]
    for copy in copies:
        copy.start()
    for copy in copies:
        copy.wait()


def pdhg_summed(dense, objective, upper_bound, power_caps, primal, dual):
    for _ in range(ITERS):
        part = jnp.dot(dual.astype(jnp.bfloat16), dense[0], preferred_element_type=jnp.float32)
        adjoint = lax.psum(part, "row")
        new = jnp.minimum(
            jnp.maximum(primal - PRIMAL_STEP * (objective[None, :] - adjoint), 0.0),
            upper_bound[None, :],
        )
        extrap = (2.0 * new - primal).astype(jnp.bfloat16)
        part = jnp.dot(extrap, dense[0].T, preferred_element_type=jnp.float32)
        forward = lax.psum(part, "col")
        dual = jnp.maximum(dual + DUAL_STEP * (power_caps - forward), 0.0)
        primal = new
    return primal, dual


def per_device(
    n_row,
    n_col,
    block_tiles,
    tile_row,
    tile_col,
    tile_count,
    objective,
    upper_bound,
    power_caps,
    primal_start,
    dual_start,
):
    block = block_tiles.shape[-1]
    cons = dual_start.shape[1]
    nvar = primal_start.shape[1]
    slots = block_tiles.shape[2]
    vectors = (objective, upper_bound, power_caps, primal_start, dual_start)
    if (
        (n_row, n_col) == (4, 4)
        and (slots, block) == (128, 128)
        and primal_start.shape[0] % 32 == 0
        and cons % (2 * block) == 0
        and nvar % (2 * block) == 0
    ):
        return pdhg(block_tiles[0, 0], tile_row[0], tile_col[0], tile_count, *vectors)
    dense = build_dense(
        block_tiles[0, 0], tile_row[0, 0], tile_col[0, 0], tile_count[0], cons, nvar, 1
    )
    return pdhg_summed(dense, *vectors)


def solution(mesh):
    return jax.shard_map(
        functools.partial(per_device, mesh.shape["row"], mesh.shape["col"]),
        mesh=mesh,
        in_specs=(
            P(("groups", "row"), "col", None, None, None),
            P(("groups", "row"), "col", None),
            P(("groups", "row"), "col", None),
            P(("groups", "row"), "col"),
            P(("groups", "col")),
            P(("groups", "col")),
            P("groups", "row"),
            P("groups", "col"),
            P("groups", "row"),
        ),
        out_specs=(P("groups", "col"), P("groups", "row")),
        check_vma=False,
    )
```

```python
import functools
import types

import jax
import jax.numpy as jnp
from jax import lax
from jax.experimental import pallas as pl
from jax.experimental.pallas import tpu as pltpu
from jax.sharding import PartitionSpec as P

ITERS = 6


PRIMAL_STEP = 0.5
DUAL_STEP = 0.2

TILE_STEP = 16
MESH = pl.DeviceIdType.MESH


def build_kernel(step_slots, rows_ref, cols_ref, count_ref, tiles_ref, k_ref):
    block = tiles_ref.shape[1]
    k_per = k_ref.shape[2] // block
    step = pl.program_id(0)

    @pl.when(step == 0)
    def _():
        k_ref[...] = jnp.zeros_like(k_ref)

    for i in range(step_slots):
        slot = step * step_slots + i

        @pl.when(slot < count_ref[0])
        def _():
            row = rows_ref[slot]
            col = cols_ref[slot]
            row_at = pl.multiple_of(row * block, block)
            k_in = pl.multiple_of(lax.rem(col, k_per) * block, block)
            k_ref[lax.div(col, k_per), pl.ds(row_at, block), pl.ds(k_in, block)] = tiles_ref[i]


def build_dense(tiles, rows, cols, count, cons, nvar, k_chunks):
    slots, block = tiles.shape[0], tiles.shape[1]
    step_slots = TILE_STEP if slots % TILE_STEP == 0 else 1
    k_shape = (k_chunks, cons, nvar // k_chunks)
    return pl.pallas_call(
        functools.partial(build_kernel, step_slots),
        out_shape=jax.ShapeDtypeStruct(k_shape, tiles.dtype),
        grid_spec=pltpu.PrefetchScalarGridSpec(
            num_scalar_prefetch=3,
            grid=(slots // step_slots,),
            in_specs=[pl.BlockSpec((step_slots, block, block), lambda t, *_: (t, 0, 0))],
            out_specs=pl.BlockSpec(k_shape, lambda t, *_: (0, 0, 0)),
        ),
        compiler_params=pltpu.CompilerParams(vmem_limit_bytes=40 << 20),
        name="build_dense",
    )(rows, cols, count, tiles)


TILE_COPIES = 8


def pdhg_kernel(
    iters,
    block,
    rows_hbm,
    cols_hbm,
    count_hbm,
    tiles_hbm,
    d0_hbm,
    p0_hbm,
    obj_hbm,
    ub_hbm,
    caps_hbm,
    p_out,
    d_out,
    rows_ref,
    cols_ref,
    count_ref,
    where_ref,
    slot_of,
    tiles_ref,
    obj_ref,
    ub_ref,
    caps_ref,
    k_ref,
    kt_ref,
    obj_wide,
    ub_wide,
    primal,
    dual,
    part,
    part_got,
    fwd,
    fwd_got,
    part_send,
    part_recv,
    pri_send,
    pri_recv,
    fwd_send,
    fwd_recv,
    dua_send,
    dua_recv,
    slot_sem,
    tile_sem,
    start_sem,
    vec_sem,
    where_sem,
):
    batches, _, rows, half_v = part.shape
    half = fwd.shape[3]
    cons = k_ref.shape[1]
    r = lax.axis_index("row")
    c = lax.axis_index("col")
    core, chip = lax.rem(c, 2), lax.div(c, 2)
    other = 1 - core
    sibling = chip * 2 + other
    across = (1 - chip) * 2 + core
    diagonal = (1 - chip) * 2 + other
    near = lax.div(r, 2)
    far = 1 - near
    inner = jnp.logical_or(r == 1, r == 2)
    outer = jnp.logical_not(inner)
    near_owner, far_owner = 1 + near, 1 + far
    near_end, far_end = 3 * near, 3 * far

    barrier = pltpu.get_barrier_semaphore()
    for k in range(1, 4):
        pl.semaphore_signal(
            barrier, inc=1, device_id={"col": lax.rem(c + k, 4)}, device_id_type=MESH
        )
    pl.semaphore_signal(
        barrier, inc=1, device_id={"row": far_owner}, device_id_type=MESH
    )

    @pl.when(inner)
    def _():
        for end in (far_end, near_end):
            pl.semaphore_signal(barrier, inc=1, device_id={"row": end}, device_id_type=MESH)

    @pl.when(outer)
    def _():
        pl.semaphore_signal(
            barrier, inc=1, device_id={"row": near_owner}, device_id_type=MESH
        )

    def rows_of(b):
        return slice(b * rows, (b + 1) * rows)

    def remote(axis, peer, src, dst, send, recv):
        width = src.shape[1]
        piece = width // 2

        def copy(at):
            return pltpu.make_async_remote_copy(
                src_ref=src.at[:, at],
                dst_ref=dst.at[:, at],
                send_sem=send,
                recv_sem=recv,
                device_id={axis: peer},
                device_id_type=MESH,
            )

        def start():
            for i in range(2):
                copy(pl.ds(i * piece, piece)).start()

        def whole():
            return copy(pl.ds(0, width))

        return types.SimpleNamespace(
            start=start,
            wait=lambda: whole().wait(),
            wait_send=lambda: whole().wait_send(),
            wait_recv=lambda: whole().wait_recv(),
        )

    def part_copy(b, which, place):
        q, owner = ((near, near_owner), (far, far_owner))[which]
        return remote(
            "row", owner, part.at[b, q], part_got.at[b, place],
            part_send.at[b, which], part_recv.at[b, place],
        )

    def pri_copy(b, k, s):
        peer = (far_end, far_owner, near_end)[k]
        return remote(
            "row", peer, primal.at[s, b, near], primal.at[s, b, near],
            pri_send.at[b, k], pri_recv.at[b, near],
        )

    def pri_arrived(b, q, s):
        pltpu.make_async_remote_copy(
            src_ref=primal.at[s, b, q],
            dst_ref=primal.at[s, b, q],
            send_sem=pri_send.at[b, 0],
            recv_sem=pri_recv.at[b, q],
            device_id={"row": far_owner},
            device_id_type=MESH,
        ).wait_recv()

    def fwd_copy(b, k, s):
        peer, q = ((sibling, other), (across, core), (diagonal, other))[k]
        return remote(
            "col", peer, fwd.at[b, q], fwd_got.at[s, b, k],
            fwd_send.at[b, k], fwd_recv.at[s, b, k],
        )

    def dua_copy(b):
        return remote(
            "col", sibling, dual.at[b, core], dual.at[b, core], dua_send.at[b], dua_recv.at[b]
        )

    def send_far(b):
        @pl.when(inner)
        def _():
            part_copy(b, 1, 1).start()

        @pl.when(outer)
        def _():
            part_copy(b, 1, 2).start()

    def send_near(b):
        @pl.when(outer)
        def _():
            part_copy(b, 0, 0).start()

    def adjoint(b, s, first=False):
        if not first:
            dua_copy(b).wait()
        low = jnp.concatenate([dual[b, 0], dual[b, 1]], axis=1).astype(jnp.bfloat16)
        part[b, far] = jnp.dot(low, k_ref[far], preferred_element_type=jnp.float32)
        send_far(b)
        part[b, near] = jnp.dot(low, k_ref[near], preferred_element_type=jnp.float32)
        send_near(b)

    def primal_step(b, s):
        @pl.when(inner)
        def _():
            part_copy(b, 0, 0).wait_recv()
            part_copy(b, 0, 1).wait_recv()
            part_copy(b, 0, 2).wait_recv()
            total = (part[b, near] + part_got[b, 0]) + (part_got[b, 1] + part_got[b, 2])
            primal[s, b, near] = jnp.minimum(
                jnp.maximum(
                    primal[1 - s, b, near] - PRIMAL_STEP * (obj_wide[near] - total), 0.0
                ),
                ub_wide[near],
            )
            for k in range(3):
                pri_copy(b, k, s).start()
            part_copy(b, 1, 1).wait_send()

        @pl.when(outer)
        def _():
            part_copy(b, 1, 2).wait_send()
            part_copy(b, 0, 0).wait_send()

    def forward(b, s):
        @pl.when(outer)
        def _():
            pri_arrived(b, near, s)

        @pl.when(inner)
        def _():
            for k in range(3):
                pri_copy(b, k, s).wait_send()

        def low(q):
            return (2.0 * primal[s, b, q] - primal[1 - s, b, q]).astype(jnp.bfloat16)

        pri_arrived(b, far, s)
        both = jnp.concatenate([low(0), low(1)], axis=1)
        sums = [
            jnp.dot(both, kt_ref[q], preferred_element_type=jnp.float32) for q in range(2)
        ]
        fwd[b, 0] = sums[0]
        fwd[b, 1] = sums[1]
        for k in (2, 0, 1):
            fwd_copy(b, k, s).start()

    own = pl.ds(pl.multiple_of(core * half, 128), half)

    def dual_step(b, s):
        for k in range(3):
            fwd_copy(b, k, s).wait()
        total = (fwd[b, core] + fwd_got[s, b, 0]) + (fwd_got[s, b, 1] + fwd_got[s, b, 2])
        dual[b, core] = jnp.maximum(
            dual[b, core] + DUAL_STEP * (caps_ref[rows_of(b), own] - total), 0.0
        )
        dua_copy(b).start()

    row_blocks, per_half, per_half_v = cons // block, half // block, half_v // block
    col_blocks = 2 * per_half_v
    slots = tiles_hbm.shape[0]

    def transpose_rows(first, last):
        def one(i, carry):
            at = pl.multiple_of(i * block, block)
            into = pl.multiple_of(lax.rem(i, per_half) * block, block)
            for j in range(col_blocks):
                inside = slice(j % per_half_v * block, (j % per_half_v + 1) * block)
                kt_ref[lax.div(i, per_half), j * block : (j + 1) * block, pl.ds(into, block)] = (
                    k_ref[j // per_half_v, pl.ds(at, block), inside].T
                )
            return carry

        lax.fori_loop(first, last, one, 0)

    def fetch(src, dst, sem):
        copy = pltpu.make_async_copy(src, dst, sem)
        copy.start()
        return copy

    slot_copies = [
        fetch(src, dst, slot_sem.at[i])
        for i, (src, dst) in enumerate(
            ((rows_hbm, rows_ref), (cols_hbm, cols_ref), (count_hbm, count_ref))
        )
    ]
    share = slots // TILE_COPIES
    tile_copies = [
        fetch(tiles_hbm.at[pl.ds(i * share, share)], tiles_ref.at[pl.ds(i * share, share)], tile_sem.at[i])
        for i in range(TILE_COPIES)
    ]
    start_copies = []
    for b in range(batches):
        for q in range(2):
            for i, (src, dst, width) in enumerate(((d0_hbm, dual, half), (p0_hbm, primal.at[1], half_v))):
                start_copies.append(
                    fetch(
                        src.at[pl.ds(b * rows, rows), pl.ds(q * width, width)],
                        dst.at[b, q],
                        start_sem.at[i, b, q],
                    )
                )
    vec_copies = [
        fetch(src, dst, vec_sem.at[i])
        for i, (src, dst) in enumerate(((obj_hbm, obj_ref), (ub_hbm, ub_ref), (caps_hbm, caps_ref)))
    ]

    tiles_ref[slots] = jnp.zeros_like(tiles_ref[slots])
    for copy in slot_copies:
        copy.wait()
    lane = lax.broadcasted_iota(jnp.int32, (slots, 128), 1)
    slot = lax.broadcasted_iota(jnp.int32, (slots, 128), 0)
    place = rows_ref[...] * col_blocks + cols_ref[...]
    place = jnp.where(lane[:1] < count_ref[...], place, -1)
    place = jnp.broadcast_to(place, (128, slots)).T
    for g in range(where_ref.shape[0]):
        found = jnp.where(place == lane + 128 * g, slot, slots)
        where_ref[g : g + 1, :] = jnp.min(found, axis=0, keepdims=True)
    where_copy = fetch(where_ref, slot_of, where_sem)
    for copy in tile_copies:
        copy.wait()
    where_copy.wait()

    def build_rows(i, carry):
        at = pl.ds(pl.multiple_of(i * block, block), block)
        for j in range(col_blocks):
            index = i * col_blocks + j
            inside = slice(j % per_half_v * block, (j % per_half_v + 1) * block)
            k_ref[j // per_half_v, at, inside] = tiles_ref[
                slot_of[lax.div(index, 128), lax.rem(index, 128)]
            ]
        return carry

    lax.fori_loop(0, row_blocks, build_rows, 0)
    for copy in start_copies:
        copy.wait()

    def transpose_part(i, s):
        transpose_rows(i * row_blocks // 6, (i + 1) * row_blocks // 6)

    def primal_out(i, s):
        for b in range(batches):
            for q in range(2):
                p_out[rows_of(b), q * half_v : (q + 1) * half_v] = primal[s, b, q]

    def dual_out(b, s):
        dua_copy(b).wait()
        for q in range(2):
            d_out[rows_of(b), q * half : (q + 1) * half] = dual[b, q]

    stages = {
        "P": primal_out, "Q": dual_out, "A": adjoint, "B": primal_step, "C": forward, "D": dual_step, "T": transpose_part
    }

    def run(order, s):
        for step in order:
            now = s if step[0].isupper() else 1 - s
            stages[step[0].upper()](int(step[1]), now)

    @pl.when(inner)
    def _():
        pl.semaphore_wait(barrier, 6)

    @pl.when(outer)
    def _():
        pl.semaphore_wait(barrier, 5)

    for b in range(batches):
        adjoint(b, 0, True)
    for copy in vec_copies:
        copy.wait()
    for j in range(col_blocks):
        at = slice(j % per_half_v * block, (j % per_half_v + 1) * block)
        obj_wide[j // per_half_v, :, at] = jnp.broadcast_to(obj_ref[j : j + 1, :], (rows, block))
        ub_wide[j // per_half_v, :, at] = jnp.broadcast_to(ub_ref[j : j + 1, :], (rows, block))
    run(FIRST, 0)

    def body(t, carry):
        run(EVERY, lax.rem(t, 2))
        return carry

    lax.fori_loop(1, iters - 1, body, 0)
    run(LAST, (iters - 1) % 2)


FIRST = ("T0", "T1", "B0", "T2", "T3", "B1", "T4", "T5", "B2", "C0", "B3", "C1", "D0", "C2")
EVERY = ("A0", "d1", "c3", "A1", "d2", "B0", "A2", "d3", "B1", "A3", "C0", "B2", "C1", "B3", "D0", "C2")
LAST = (
    "A0", "d1", "c3", "A1", "d2", "B0", "A2", "d3", "B1", "A3", "C0", "B2", "B3", "C1", "C2", "D0", "C3", "D1", "P0", "D2", "Q0", "Q1", "Q2", "D3", "Q3",
)


def pdhg(
    tiles, rows, cols, count, objective, upper_bound, power_caps, primal_start, dual_start
):
    slots, block = tiles.shape[0], tiles.shape[1]
    scenarios, nvar = primal_start.shape
    cons = dual_start.shape[1]
    half, half_v = cons // 2, nvar // 2
    batches, rows_batch = 4, scenarios // 4
    places = pl.cdiv((cons // block) * (nvar // block), 128)
    hbm = pl.BlockSpec(memory_space=pltpu.HBM)
    vmem = pl.BlockSpec(memory_space=pltpu.VMEM)
    f32 = jnp.float32
    var_shape = (batches, 2, rows_batch, half_v)
    con_shape = (batches, 2, rows_batch, half)
    dma = pltpu.SemaphoreType.DMA
    outs = pl.pallas_call(
        functools.partial(pdhg_kernel, ITERS, block),
        out_shape=(pltpu.VMEM((scenarios, nvar), f32), pltpu.VMEM((scenarios, cons), f32)),
        in_specs=[hbm] * 9,
        out_specs=(vmem, vmem),
        scratch_shapes=[
            pltpu.VMEM(rows.shape, rows.dtype),
            pltpu.VMEM(cols.shape, cols.dtype),
            pltpu.VMEM(count.shape, count.dtype),
            pltpu.VMEM((places, 128), jnp.int32),
            pltpu.SMEM((places, 128), jnp.int32),
            pltpu.VMEM((slots + 1, block, block), tiles.dtype),
            pltpu.VMEM((nvar // block, block), f32),
            pltpu.VMEM((nvar // block, block), f32),
            pltpu.VMEM(power_caps.shape, f32),
            pltpu.VMEM((2, cons, half_v), tiles.dtype),
            pltpu.VMEM((2, nvar, half), tiles.dtype),
            pltpu.VMEM((2, rows_batch, half_v), f32),
            pltpu.VMEM((2, rows_batch, half_v), f32),
            pltpu.VMEM((2, *var_shape), f32),
            pltpu.VMEM(con_shape, f32),
            pltpu.VMEM(var_shape, f32),
            pltpu.VMEM((batches, 3, rows_batch, half_v), f32),
            pltpu.VMEM(con_shape, f32),
            pltpu.VMEM((2, batches, 3, rows_batch, half), f32),
            dma((batches, 2)),
            dma((batches, 3)),
            dma((batches, 3)),
            dma((batches, 2)),
            dma((batches, 3)),
            dma((2, batches, 3)),
            dma((batches,)),
            dma((batches,)),
            dma((3,)),
            dma((TILE_COPIES,)),
            dma((2, batches, 2)),
            dma((3,)),
            dma,
        ],
        compiler_params=pltpu.CompilerParams(
            collective_id=0, has_side_effects=True, vmem_limit_bytes=60 << 20
        ),
        name="pdhg",
    )(
        rows,
        cols,
        count,
        tiles,
        dual_start,
        primal_start,
        objective.reshape(-1, block),
        upper_bound.reshape(-1, block),
        power_caps,
    )
    return pl.pallas_call(
        store_kernel,
        out_shape=(
            jax.ShapeDtypeStruct((scenarios, nvar), f32),
            jax.ShapeDtypeStruct((scenarios, cons), f32),
        ),
        in_specs=[vmem] * 2,
        out_specs=(hbm, hbm),
        scratch_shapes=[dma((2,))],
        compiler_params=pltpu.CompilerParams(vmem_limit_bytes=4 << 20),
        name="store",
    )(*outs)


def store_kernel(p_ref, d_ref, p_out, d_out, sem):
    copies = [
        pltpu.make_async_copy(src, dst, sem.at[i])
        for i, (src, dst) in enumerate(((p_ref, p_out), (d_ref, d_out)))
    ]
    for copy in copies:
        copy.start()
    for copy in copies:
        copy.wait()


def pdhg_summed(dense, objective, upper_bound, power_caps, primal, dual):
    for _ in range(ITERS):
        part = jnp.dot(dual.astype(jnp.bfloat16), dense[0], preferred_element_type=jnp.float32)
        adjoint = lax.psum(part, "row")
        new = jnp.minimum(
            jnp.maximum(primal - PRIMAL_STEP * (objective[None, :] - adjoint), 0.0),
            upper_bound[None, :],
        )
        extrap = (2.0 * new - primal).astype(jnp.bfloat16)
        part = jnp.dot(extrap, dense[0].T, preferred_element_type=jnp.float32)
        forward = lax.psum(part, "col")
        dual = jnp.maximum(dual + DUAL_STEP * (power_caps - forward), 0.0)
        primal = new
    return primal, dual


def per_device(
    n_row,
    n_col,
    block_tiles,
    tile_row,
    tile_col,
    tile_count,
    objective,
    upper_bound,
    power_caps,
    primal_start,
    dual_start,
):
    block = block_tiles.shape[-1]
    cons = dual_start.shape[1]
    nvar = primal_start.shape[1]
    slots = block_tiles.shape[2]
    vectors = (objective, upper_bound, power_caps, primal_start, dual_start)
    if (
        (n_row, n_col) == (4, 4)
        and (slots, block) == (128, 128)
        and primal_start.shape[0] % 32 == 0
        and cons % (2 * block) == 0
        and nvar % (2 * block) == 0
    ):
        return pdhg(block_tiles[0, 0], tile_row[0], tile_col[0], tile_count, *vectors)
    dense = build_dense(
        block_tiles[0, 0], tile_row[0, 0], tile_col[0, 0], tile_count[0], cons, nvar, 1
    )
    return pdhg_summed(dense, *vectors)


def solution(mesh):
    return jax.shard_map(
        functools.partial(per_device, mesh.shape["row"], mesh.shape["col"]),
        mesh=mesh,
        in_specs=(
            P(("groups", "row"), "col", None, None, None),
            P(("groups", "row"), "col", None),
            P(("groups", "row"), "col", None),
            P(("groups", "row"), "col"),
            P(("groups", "col")),
            P(("groups", "col")),
            P("groups", "row"),
            P("groups", "col"),
            P("groups", "row"),
        ),
        out_specs=(P("groups", "col"), P("groups", "row")),
        check_vma=False,
    )
```

```python
import functools
import types

import jax
import jax.numpy as jnp
from jax import lax
from jax.experimental import pallas as pl
from jax.experimental.pallas import tpu as pltpu
from jax.sharding import PartitionSpec as P

ITERS = 6


PRIMAL_STEP = 0.5
DUAL_STEP = 0.2

TILE_STEP = 16
MESH = pl.DeviceIdType.MESH


def build_kernel(step_slots, rows_ref, cols_ref, count_ref, tiles_ref, k_ref):
    block = tiles_ref.shape[1]
    k_per = k_ref.shape[2] // block
    step = pl.program_id(0)

    @pl.when(step == 0)
    def _():
        k_ref[...] = jnp.zeros_like(k_ref)

    for i in range(step_slots):
        slot = step * step_slots + i

        @pl.when(slot < count_ref[0])
        def _():
            row = rows_ref[slot]
            col = cols_ref[slot]
            row_at = pl.multiple_of(row * block, block)
            k_in = pl.multiple_of(lax.rem(col, k_per) * block, block)
            k_ref[lax.div(col, k_per), pl.ds(row_at, block), pl.ds(k_in, block)] = tiles_ref[i]


def build_dense(tiles, rows, cols, count, cons, nvar, k_chunks):
    slots, block = tiles.shape[0], tiles.shape[1]
    step_slots = TILE_STEP if slots % TILE_STEP == 0 else 1
    k_shape = (k_chunks, cons, nvar // k_chunks)
    return pl.pallas_call(
        functools.partial(build_kernel, step_slots),
        out_shape=jax.ShapeDtypeStruct(k_shape, tiles.dtype),
        grid_spec=pltpu.PrefetchScalarGridSpec(
            num_scalar_prefetch=3,
            grid=(slots // step_slots,),
            in_specs=[pl.BlockSpec((step_slots, block, block), lambda t, *_: (t, 0, 0))],
            out_specs=pl.BlockSpec(k_shape, lambda t, *_: (0, 0, 0)),
        ),
        compiler_params=pltpu.CompilerParams(vmem_limit_bytes=40 << 20),
        name="build_dense",
    )(rows, cols, count, tiles)


TILE_COPIES = 8


def pdhg_kernel(
    iters,
    block,
    rows_hbm,
    cols_hbm,
    count_hbm,
    tiles_hbm,
    d0_hbm,
    p0_hbm,
    obj_hbm,
    ub_hbm,
    caps_hbm,
    p_out,
    d_out,
    rows_ref,
    cols_ref,
    count_ref,
    where_ref,
    slot_of,
    tiles_ref,
    obj_ref,
    ub_ref,
    caps_ref,
    k_ref,
    kt_ref,
    obj_wide,
    ub_wide,
    primal,
    dual,
    part,
    part_got,
    fwd,
    fwd_got,
    part_send,
    part_recv,
    pri_send,
    pri_recv,
    fwd_send,
    fwd_recv,
    dua_send,
    dua_recv,
    slot_sem,
    tile_sem,
    start_sem,
    vec_sem,
    where_sem,
):
    batches, _, rows, half_v = part.shape
    half = fwd.shape[3]
    cons = k_ref.shape[1]
    r = lax.axis_index("row")
    c = lax.axis_index("col")
    core, chip = lax.rem(c, 2), lax.div(c, 2)
    other = 1 - core
    sibling = chip * 2 + other
    across = (1 - chip) * 2 + core
    diagonal = (1 - chip) * 2 + other
    near = lax.div(r, 2)
    far = 1 - near
    inner = jnp.logical_or(r == 1, r == 2)
    outer = jnp.logical_not(inner)
    near_owner, far_owner = 1 + near, 1 + far
    near_end, far_end = 3 * near, 3 * far

    barrier = pltpu.get_barrier_semaphore()
    for k in range(1, 4):
        pl.semaphore_signal(
            barrier, inc=1, device_id={"col": lax.rem(c + k, 4)}, device_id_type=MESH
        )
    pl.semaphore_signal(
        barrier, inc=1, device_id={"row": far_owner}, device_id_type=MESH
    )

    @pl.when(inner)
    def _():
        for end in (far_end, near_end):
            pl.semaphore_signal(barrier, inc=1, device_id={"row": end}, device_id_type=MESH)

    @pl.when(outer)
    def _():
        pl.semaphore_signal(
            barrier, inc=1, device_id={"row": near_owner}, device_id_type=MESH
        )

    def rows_of(b):
        return slice(b * rows, (b + 1) * rows)

    def remote(axis, peer, src, dst, send, recv):
        width = src.shape[1]
        piece = width // 2

        def copy(at):
            return pltpu.make_async_remote_copy(
                src_ref=src.at[:, at],
                dst_ref=dst.at[:, at],
                send_sem=send,
                recv_sem=recv,
                device_id={axis: peer},
                device_id_type=MESH,
            )

        def start():
            for i in range(2):
                copy(pl.ds(i * piece, piece)).start()

        def whole():
            return copy(pl.ds(0, width))

        return types.SimpleNamespace(
            start=start,
            wait=lambda: whole().wait(),
            wait_send=lambda: whole().wait_send(),
            wait_recv=lambda: whole().wait_recv(),
        )

    def part_copy(b, which, place):
        q, owner = ((near, near_owner), (far, far_owner))[which]
        return remote(
            "row", owner, part.at[b, q], part_got.at[b, place],
            part_send.at[b, which], part_recv.at[b, place],
        )

    def pri_copy(b, k, s):
        peer = (far_end, far_owner, near_end)[k]
        return remote(
            "row", peer, primal.at[s, b, near], primal.at[s, b, near],
            pri_send.at[b, k], pri_recv.at[b, near],
        )

    def pri_arrived(b, q, s):
        pltpu.make_async_remote_copy(
            src_ref=primal.at[s, b, q],
            dst_ref=primal.at[s, b, q],
            send_sem=pri_send.at[b, 0],
            recv_sem=pri_recv.at[b, q],
            device_id={"row": far_owner},
            device_id_type=MESH,
        ).wait_recv()

    def fwd_copy(b, k, s):
        peer, q = ((sibling, other), (across, core), (diagonal, other))[k]
        return remote(
            "col", peer, fwd.at[b, q], fwd_got.at[s, b, k],
            fwd_send.at[b, k], fwd_recv.at[s, b, k],
        )

    def dua_copy(b):
        return remote(
            "col", sibling, dual.at[b, core], dual.at[b, core], dua_send.at[b], dua_recv.at[b]
        )

    def send_far(b):
        @pl.when(inner)
        def _():
            part_copy(b, 1, 1).start()

        @pl.when(outer)
        def _():
            part_copy(b, 1, 2).start()

    def send_near(b):
        @pl.when(outer)
        def _():
            part_copy(b, 0, 0).start()

    def adjoint(b, s, first=False, between=lambda: None):
        if not first:
            dua_copy(b).wait()
        low = jnp.concatenate([dual[b, 0], dual[b, 1]], axis=1).astype(jnp.bfloat16)
        part[b, far] = jnp.dot(low, k_ref[far], preferred_element_type=jnp.float32)
        send_far(b)
        between()
        part[b, near] = jnp.dot(low, k_ref[near], preferred_element_type=jnp.float32)
        send_near(b)

    def primal_step(b, s):
        @pl.when(inner)
        def _():
            part_copy(b, 0, 0).wait_recv()
            part_copy(b, 0, 1).wait_recv()
            part_copy(b, 0, 2).wait_recv()
            total = (part[b, near] + part_got[b, 0]) + (part_got[b, 1] + part_got[b, 2])
            primal[s, b, near] = jnp.minimum(
                jnp.maximum(
                    primal[1 - s, b, near] - PRIMAL_STEP * (obj_wide[near] - total), 0.0
                ),
                ub_wide[near],
            )
            for k in range(3):
                pri_copy(b, k, s).start()
            part_copy(b, 1, 1).wait_send()

        @pl.when(outer)
        def _():
            part_copy(b, 1, 2).wait_send()
            part_copy(b, 0, 0).wait_send()

    def forward(b, s):
        @pl.when(outer)
        def _():
            pri_arrived(b, near, s)

        @pl.when(inner)
        def _():
            for k in range(3):
                pri_copy(b, k, s).wait_send()

        def low(q):
            return (2.0 * primal[s, b, q] - primal[1 - s, b, q]).astype(jnp.bfloat16)

        pri_arrived(b, far, s)
        both = jnp.concatenate([low(0), low(1)], axis=1)
        sums = [
            jnp.dot(both, kt_ref[q], preferred_element_type=jnp.float32) for q in range(2)
        ]
        fwd[b, 0] = sums[0]
        fwd[b, 1] = sums[1]
        for k in (2, 0, 1):
            fwd_copy(b, k, s).start()

    own = pl.ds(pl.multiple_of(core * half, 128), half)

    def dual_step(b, s):
        for k in range(3):
            fwd_copy(b, k, s).wait()
        total = (fwd[b, core] + fwd_got[s, b, 0]) + (fwd_got[s, b, 1] + fwd_got[s, b, 2])
        dual[b, core] = jnp.maximum(
            dual[b, core] + DUAL_STEP * (caps_ref[rows_of(b), own] - total), 0.0
        )
        dua_copy(b).start()

    row_blocks, per_half, per_half_v = cons // block, half // block, half_v // block
    col_blocks = 2 * per_half_v
    slots = tiles_hbm.shape[0]

    def transpose_rows(first, last):
        def one(i, carry):
            at = pl.multiple_of(i * block, block)
            into = pl.multiple_of(lax.rem(i, per_half) * block, block)
            for j in range(col_blocks):
                inside = slice(j % per_half_v * block, (j % per_half_v + 1) * block)
                kt_ref[lax.div(i, per_half), j * block : (j + 1) * block, pl.ds(into, block)] = (
                    k_ref[j // per_half_v, pl.ds(at, block), inside].T
                )
            return carry

        lax.fori_loop(first, last, one, 0)

    def fetch(src, dst, sem):
        copy = pltpu.make_async_copy(src, dst, sem)
        copy.start()
        return copy

    slot_copies = [
        fetch(src, dst, slot_sem.at[i])
        for i, (src, dst) in enumerate(
            ((rows_hbm, rows_ref), (cols_hbm, cols_ref), (count_hbm, count_ref))
        )
    ]
    share = slots // TILE_COPIES
    tile_copies = [
        fetch(tiles_hbm.at[pl.ds(i * share, share)], tiles_ref.at[pl.ds(i * share, share)], tile_sem.at[i])
        for i in range(TILE_COPIES)
    ]
    start_copies = []
    for b in range(batches):
        for q in range(2):
            for i, (src, dst, width) in enumerate(((d0_hbm, dual, half), (p0_hbm, primal.at[1], half_v))):
                start_copies.append(
                    fetch(
                        src.at[pl.ds(b * rows, rows), pl.ds(q * width, width)],
                        dst.at[b, q],
                        start_sem.at[i, b, q],
                    )
                )
    vec_copies = [
        fetch(src, dst, vec_sem.at[i])
        for i, (src, dst) in enumerate(((obj_hbm, obj_ref), (ub_hbm, ub_ref), (caps_hbm, caps_ref)))
    ]

    tiles_ref[slots] = jnp.zeros_like(tiles_ref[slots])
    for copy in slot_copies:
        copy.wait()
    lane = lax.broadcasted_iota(jnp.int32, (slots, 128), 1)
    slot = lax.broadcasted_iota(jnp.int32, (slots, 128), 0)
    place = rows_ref[...] * col_blocks + cols_ref[...]
    place = jnp.where(lane[:1] < count_ref[...], place, -1)
    place = jnp.broadcast_to(place, (128, slots)).T
    for g in range(where_ref.shape[0]):
        found = jnp.where(place == lane + 128 * g, slot, slots)
        where_ref[g : g + 1, :] = jnp.min(found, axis=0, keepdims=True)
    where_copy = fetch(where_ref, slot_of, where_sem)
    for copy in tile_copies:
        copy.wait()
    where_copy.wait()

    def build_half(q):
        def one(i, carry):
            at = pl.ds(pl.multiple_of(i * block, block), block)
            for j in range(per_half_v):
                index = i * col_blocks + q * per_half_v + j
                k_ref[q, at, j * block : (j + 1) * block] = tiles_ref[
                    slot_of[lax.div(index, 128), lax.rem(index, 128)]
                ]
            return carry

        lax.fori_loop(0, row_blocks, one, 0)

    build_half(far)
    for copy in start_copies:
        copy.wait()

    def transpose_part(i, s):
        transpose_rows(i * row_blocks // 6, (i + 1) * row_blocks // 6)

    def primal_out(i, s):
        for b in range(batches):
            for q in range(2):
                p_out[rows_of(b), q * half_v : (q + 1) * half_v] = primal[s, b, q]

    def dual_out(b, s):
        dua_copy(b).wait()
        for q in range(2):
            d_out[rows_of(b), q * half : (q + 1) * half] = dual[b, q]

    stages = {
        "P": primal_out, "Q": dual_out, "A": adjoint, "B": primal_step, "C": forward, "D": dual_step, "T": transpose_part
    }

    def run(order, s):
        for step in order:
            now = s if step[0].isupper() else 1 - s
            stages[step[0].upper()](int(step[1]), now)

    @pl.when(inner)
    def _():
        pl.semaphore_wait(barrier, 6)

    @pl.when(outer)
    def _():
        pl.semaphore_wait(barrier, 5)

    adjoint(0, 0, True, lambda: build_half(near))
    for b in range(1, batches):
        adjoint(b, 0, True)
    for copy in vec_copies:
        copy.wait()
    for j in range(col_blocks):
        at = slice(j % per_half_v * block, (j % per_half_v + 1) * block)
        obj_wide[j // per_half_v, :, at] = jnp.broadcast_to(obj_ref[j : j + 1, :], (rows, block))
        ub_wide[j // per_half_v, :, at] = jnp.broadcast_to(ub_ref[j : j + 1, :], (rows, block))
    run(FIRST, 0)

    def body(t, carry):
        run(EVERY, lax.rem(t, 2))
        return carry

    lax.fori_loop(1, iters - 1, body, 0)
    run(LAST, (iters - 1) % 2)


FIRST = ("T0", "T1", "B0", "T2", "T3", "B1", "T4", "T5", "B2", "C0", "B3", "C1", "D0", "C2")
EVERY = ("A0", "d1", "c3", "A1", "d2", "B0", "A2", "d3", "B1", "A3", "C0", "B2", "C1", "B3", "D0", "C2")
LAST = (
    "A0", "d1", "c3", "A1", "d2", "B0", "A2", "d3", "B1", "A3", "C0", "B2", "B3", "C1", "C2", "D0", "C3", "D1", "P0", "D2", "Q0", "Q1", "Q2", "D3", "Q3",
)


def pdhg(
    tiles, rows, cols, count, objective, upper_bound, power_caps, primal_start, dual_start
):
    slots, block = tiles.shape[0], tiles.shape[1]
    scenarios, nvar = primal_start.shape
    cons = dual_start.shape[1]
    half, half_v = cons // 2, nvar // 2
    batches, rows_batch = 4, scenarios // 4
    places = pl.cdiv((cons // block) * (nvar // block), 128)
    hbm = pl.BlockSpec(memory_space=pltpu.HBM)
    vmem = pl.BlockSpec(memory_space=pltpu.VMEM)
    f32 = jnp.float32
    var_shape = (batches, 2, rows_batch, half_v)
    con_shape = (batches, 2, rows_batch, half)
    dma = pltpu.SemaphoreType.DMA
    outs = pl.pallas_call(
        functools.partial(pdhg_kernel, ITERS, block),
        out_shape=(pltpu.VMEM((scenarios, nvar), f32), pltpu.VMEM((scenarios, cons), f32)),
        in_specs=[hbm] * 9,
        out_specs=(vmem, vmem),
        scratch_shapes=[
            pltpu.VMEM(rows.shape, rows.dtype),
            pltpu.VMEM(cols.shape, cols.dtype),
            pltpu.VMEM(count.shape, count.dtype),
            pltpu.VMEM((places, 128), jnp.int32),
            pltpu.SMEM((places, 128), jnp.int32),
            pltpu.VMEM((slots + 1, block, block), tiles.dtype),
            pltpu.VMEM((nvar // block, block), f32),
            pltpu.VMEM((nvar // block, block), f32),
            pltpu.VMEM(power_caps.shape, f32),
            pltpu.VMEM((2, cons, half_v), tiles.dtype),
            pltpu.VMEM((2, nvar, half), tiles.dtype),
            pltpu.VMEM((2, rows_batch, half_v), f32),
            pltpu.VMEM((2, rows_batch, half_v), f32),
            pltpu.VMEM((2, *var_shape), f32),
            pltpu.VMEM(con_shape, f32),
            pltpu.VMEM(var_shape, f32),
            pltpu.VMEM((batches, 3, rows_batch, half_v), f32),
            pltpu.VMEM(con_shape, f32),
            pltpu.VMEM((2, batches, 3, rows_batch, half), f32),
            dma((batches, 2)),
            dma((batches, 3)),
            dma((batches, 3)),
            dma((batches, 2)),
            dma((batches, 3)),
            dma((2, batches, 3)),
            dma((batches,)),
            dma((batches,)),
            dma((3,)),
            dma((TILE_COPIES,)),
            dma((2, batches, 2)),
            dma((3,)),
            dma,
        ],
        compiler_params=pltpu.CompilerParams(
            collective_id=0, has_side_effects=True, vmem_limit_bytes=60 << 20
        ),
        name="pdhg",
    )(
        rows,
        cols,
        count,
        tiles,
        dual_start,
        primal_start,
        objective.reshape(-1, block),
        upper_bound.reshape(-1, block),
        power_caps,
    )
    return pl.pallas_call(
        store_kernel,
        out_shape=(
            jax.ShapeDtypeStruct((scenarios, nvar), f32),
            jax.ShapeDtypeStruct((scenarios, cons), f32),
        ),
        in_specs=[vmem] * 2,
        out_specs=(hbm, hbm),
        scratch_shapes=[dma((2,))],
        compiler_params=pltpu.CompilerParams(vmem_limit_bytes=4 << 20),
        name="store",
    )(*outs)


def store_kernel(p_ref, d_ref, p_out, d_out, sem):
    copies = [
        pltpu.make_async_copy(src, dst, sem.at[i])
        for i, (src, dst) in enumerate(((p_ref, p_out), (d_ref, d_out)))
    ]
    for copy in copies:
        copy.start()
    for copy in copies:
        copy.wait()


def pdhg_summed(dense, objective, upper_bound, power_caps, primal, dual):
    for _ in range(ITERS):
        part = jnp.dot(dual.astype(jnp.bfloat16), dense[0], preferred_element_type=jnp.float32)
        adjoint = lax.psum(part, "row")
        new = jnp.minimum(
            jnp.maximum(primal - PRIMAL_STEP * (objective[None, :] - adjoint), 0.0),
            upper_bound[None, :],
        )
        extrap = (2.0 * new - primal).astype(jnp.bfloat16)
        part = jnp.dot(extrap, dense[0].T, preferred_element_type=jnp.float32)
        forward = lax.psum(part, "col")
        dual = jnp.maximum(dual + DUAL_STEP * (power_caps - forward), 0.0)
        primal = new
    return primal, dual


def per_device(
    n_row,
    n_col,
    block_tiles,
    tile_row,
    tile_col,
    tile_count,
    objective,
    upper_bound,
    power_caps,
    primal_start,
    dual_start,
):
    block = block_tiles.shape[-1]
    cons = dual_start.shape[1]
    nvar = primal_start.shape[1]
    slots = block_tiles.shape[2]
    vectors = (objective, upper_bound, power_caps, primal_start, dual_start)
    if (
        (n_row, n_col) == (4, 4)
        and (slots, block) == (128, 128)
        and primal_start.shape[0] % 32 == 0
        and cons % (2 * block) == 0
        and nvar % (2 * block) == 0
    ):
        return pdhg(block_tiles[0, 0], tile_row[0], tile_col[0], tile_count, *vectors)
    dense = build_dense(
        block_tiles[0, 0], tile_row[0, 0], tile_col[0, 0], tile_count[0], cons, nvar, 1
    )
    return pdhg_summed(dense, *vectors)


def solution(mesh):
    return jax.shard_map(
        functools.partial(per_device, mesh.shape["row"], mesh.shape["col"]),
        mesh=mesh,
        in_specs=(
            P(("groups", "row"), "col", None, None, None),
            P(("groups", "row"), "col", None),
            P(("groups", "row"), "col", None),
            P(("groups", "row"), "col"),
            P(("groups", "col")),
            P(("groups", "col")),
            P("groups", "row"),
            P("groups", "col"),
            P("groups", "row"),
        ),
        out_specs=(P("groups", "col"), P("groups", "row")),
        check_vma=False,
    )
```
